256 devices in a mesh: dp: 256 (over x, y, z, core).
Axes of the slice: x: 4, y: 4, z: 8, core: 2. Of those that a mesh axis runs over, the one named last changes fastest.
Arguments:
- bin_index: int32 [524288, 256], P('dp'), may hold values from 0 to 63
- node_ids: int32 [524288], P('dp'), may hold values from 0 to 1
- gradients: bfloat16 [524288, 32], P('dp'), may hold values from -6 to 6
- hessians: bfloat16 [524288, 32], P('dp'), may hold values from 0.02 to 0.25
Outputs:
- gains: float32 [256, 2, 64], replicated
- weights: float32 [256, 2, 64, 32], replicated
The draws below stay inside these ranges and needn't reach their ends.
All inputs are finite; a program needn't handle non-finite values.
Results may differ from the reference program's by a relative error of at most 0.0003.
Values sent between devices are 32-bit elements; how exact they have to be, the bound alone decides.
A program may use at most 128 MiB of HBM per device.

```python
import math
import jax
import jax.numpy as jnp
from jax import lax

F = 256
B = 64
K = 32
NODES = 2
ROWS = 524288


def latent_level(key):
    row_order = jax.random.permutation(jax.random.fold_in(key, 11), ROWS).astype(jnp.int32)
    row_level = (row_order % B).astype(jnp.int32)
    return (row_order, row_level)


def draw_bin_index(key, part):
    row_order, row_level = latent_level(key)
    subkeys = jax.random.split(jax.random.fold_in(key, 23), 3)
    strides = 2 * jax.random.randint(subkeys[0], (F,), 0, B // 2) + 1
    offsets = jax.random.randint(subkeys[1], (F,), 0, B)
    jitters = jax.random.randint(subkeys[2], (ROWS, F), 0, max(B // 4, 2))
    jitters = jitters * (row_order >= B).astype(jnp.int32)[:, None]
    mixed = row_level[:, None] * strides[None, :] + offsets[None, :] + jitters
    return (mixed % B).astype(jnp.int32)


def draw_hessians(key, part):
    row_order, row_level = latent_level(key)
    subkeys = jax.random.split(jax.random.fold_in(key, 31), 2)
    level_table = jnp.exp(jax.random.uniform(subkeys[0], (B, K), jnp.float32, math.log(0.03), math.log(0.2)))
    row_factor = jax.random.uniform(subkeys[1], (ROWS, K), jnp.float32, 0.75, 1.2)
    values = level_table[row_level] * row_factor
    return values.astype(jnp.bfloat16)


def plant(array, rng, low, high):
    longest = array.shape.index(max(array.shape))
    spots = []
    for shift in (0, 1):
        where = [jax.random.randint(jax.random.fold_in(rng, axis), (), 0, length) for axis, length in enumerate(array.shape)]
        where[longest] = (where[longest] + shift) % array.shape[longest]
        spots.append(tuple(where))
    return array.at[spots[0]].set(low).at[spots[1]].set(high)


def shard_levels(own_key, dims, pieces, low, largest):
    gain, own = 1.0, jax.random.fold_in(own_key, 6)
    for position, blocks in pieces:
        steps = jnp.exp(jax.random.uniform(jax.random.fold_in(own, position), (blocks,), jnp.float32, low / len(pieces), largest / len(pieces)))
        gain = gain * jnp.repeat(steps, dims[position] // blocks).reshape([-1 if axis == position else 1 for axis in range(len(dims))])
    return gain


def gaussian(stream_key, dims, scale, most, shards=(), held_as=jnp.bfloat16):
    values = jax.random.normal(stream_key, dims, jnp.float32) * scale
    if len(shards) > 0:
        values = shard_levels(stream_key, dims, shards, -0.22, 0.18) * values
    return jnp.clip(values, min=-most, max=most).astype(held_as)


def setup_inputs(seed: int = 0) -> dict:
    seeds = jax.random.split(jax.random.key(seed), 5)
    return {
        "bin_index": draw_bin_index(jax.random.fold_in(seeds[4], 71), 0),
        "node_ids": plant(jax.random.randint(seeds[1], (ROWS,), 0, NODES), jax.random.fold_in(seeds[1], 1), 0, NODES - 1).astype(jnp.int32),
        "gradients": gaussian(seeds[2], (ROWS, K), 1.0, 6.0, ((0, 256),)),
        "hessians": draw_hessians(jax.random.fold_in(seeds[4], 71), 0),
    }


RIDGE = 1.0


def curves(hist):
    width = hist.shape[-1] // 2
    running = jnp.cumsum(hist, axis=2)
    totals = running[:, :, -1:, :]
    right_side = totals - running

    def score(part):
        return part[..., :width] * part[..., :width] / (part[..., width:] + RIDGE)

    gains = jnp.mean(score(running) + score(right_side) - score(totals), axis=-1)
    weights = -running[..., :width] / (running[..., width:] + RIDGE)
    return gains, weights


def reference(bin_index, node_ids, gradients, hessians):
    paired = jnp.concatenate([gradients, hessians], axis=1).astype(jnp.float32)

    def one_feature(column):
        segment = (node_ids * B + column).astype(jnp.int32)
        summed = jax.ops.segment_sum(paired, segment, num_segments=NODES * B)
        return summed.reshape(NODES, B, 2 * K)

    hist = lax.map(one_feature, bin_index.T)
    gains, weights = curves(hist)
    return gains, weights
```

```python
import functools

import jax
import jax.numpy as jnp
from jax import lax
from jax.experimental import pallas as pl
from jax.experimental.pallas import tpu as pltpu
from jax.sharding import PartitionSpec as P

MESH = pl.DeviceIdType.MESH

BINS = 64
TARGETS = 32
WIDE = 2 * TARGETS
LANES = 128
NX, NY, NZ = 4, 4, 8
PLANE = NX * NY
RIDGE = 1.0
DEPTH = 1024
ROWS_OUT = 4 * WIDE
MESSAGE = ROWS_OUT + 8
PIECE = WIDE + 8
SHARE = TARGETS + 8
PACK = 4 * TARGETS + 8


def offset(u):
    high, low = u // 2, u % 2
    return (2 + low) * (1 - high) + (1 - low) * high


def kernel(
    rows,
    bins_hbm,
    node_ref,
    grad_ref,
    hess_ref,
    weights_ref,
    gains_ref,
    bins,
    spread,
    mine,
    theirs,
    tot,
    sent,
    got,
    zsent,
    zgot,
    share,
    pack,
    mate,
    own_sem,
    pair_send,
    pair_recv,
    send_sem,
    recv_sem,
    zsend_sem,
    zrecv_sem,
    ssend_sem,
    srecv_sem,
    psend_sem,
    precv_sem,
    msend_sem,
    mrecv_sem,
):
    me = lax.axis_index("dp")
    core = me % 2
    z = (me // 2) % NZ
    y = (me // (2 * NZ)) % NY
    x = me // (2 * NZ * NY)
    sign = 1 - 2 * core
    other = 1 - core
    mate_id = me + sign

    def device(kind, a, b, zz):
        xx, yy = (b, a) if kind == 0 else (a, b)
        return ((xx * NY + yy) * NZ + zz) * 2 + core

    def place(kind):
        return (y, x) if kind == 0 else (x, y)

    def step(p, d):
        return (p + d + 8) % 4

    def remote(src, dst, send, recv, target):
        copy = pltpu.make_async_remote_copy(
            src_ref=src, dst_ref=dst, send_sem=send, recv_sem=recv, device_id=(target,), device_id_type=MESH
        )
        return copy

    own_lanes = pl.ds(pl.multiple_of(core * LANES, LANES), LANES)
    mate_lanes = pl.ds(pl.multiple_of(other * LANES, LANES), LANES)
    own_bins = pltpu.make_async_copy(bins_hbm.at[:, own_lanes], bins.at[pl.ds(0, rows)], own_sem.at[0])
    own_bins.start()

    barrier = pltpu.get_barrier_semaphore()
    greeted = [mate_id]
    for kind in (0, 1):
        a, b = place(kind)
        greeted += [device(kind, a, step(b, 1), z), device(kind, a, step(b, -1), z)]
    for d in range(1, NZ):
        greeted.append(device(0, y, x, (z + d) % NZ))
    for peer in greeted:
        pl.semaphore_signal(barrier, inc=1, device_id=(peer,), device_id_type=MESH)

    nodes = node_ref[...].astype(jnp.float32)
    grads = grad_ref[...].astype(jnp.float32)
    hesss = hess_ref[...].astype(jnp.float32)
    mine[0:TARGETS, :] = grads
    mine[TARGETS:WIDE, :] = hesss
    mine[WIDE:PIECE, :] = jnp.broadcast_to(nodes, (8, rows))

    pl.semaphore_wait(barrier, len(greeted))

    pair_bins = remote(bins_hbm.at[:, mate_lanes], bins.at[pl.ds(rows, rows)], pair_send.at[0], pair_recv.at[0], mate_id)
    pair_vals = remote(mine, theirs, pair_send.at[1], pair_recv.at[1], mate_id)
    pair_vals.start()
    pair_bins.start()

    def fill(values, start):
        which = values[WIDE : WIDE + 1, :]
        both = values[0:WIDE, :]
        for n in (0, 1):
            part = jnp.where(which == float(n), both, 0.0)
            spread[n * WIDE : (n + 1) * WIDE, start : start + rows] = part.astype(jnp.bfloat16)

    fill(mine, 0)
    pair_vals.wait_recv()
    fill(theirs, rows)
    ones = jnp.ones((8, 2 * rows), jnp.bfloat16)
    tot[...] = lax.dot_general(ones, spread[...], (((1,), (1,)), ((), ())), preferred_element_type=jnp.float32)
    own_bins.wait()
    pair_bins.wait_recv()

    def local(t, u):
        firsts = []
        for kind in (0, 1):
            a, b = place(kind)
            firsts.append(kind * 32 + step(b, offset(t) * sign) * 8 + step(a, offset(u) * sign) * 2)
        total = None
        for start in range(0, 2 * rows, DEPTH):
            block = bins[start : start + DEPTH, :]
            hot = [
                jnp.where(block <= first + j, jnp.ones((), jnp.bfloat16), jnp.zeros((), jnp.bfloat16))
                for first in firsts
                for j in (0, 1)
            ]
            term = jnp.dot(
                spread[:, start : start + DEPTH], jnp.concatenate(hot, axis=1), preferred_element_type=jnp.float32
            )
            total = term if total is None else total + term
        return total

    def message(m, kind, target):
        return remote(sent.at[m, kind], got.at[m, kind], send_sem.at[m, kind], recv_sem.at[m, kind], target)

    def arrived(m, kind):
        message(m, kind, me).wait_recv()

    def piece(total, kind, j, extra):
        value = total[:, (2 * kind + j) * LANES : (2 * kind + j + 1) * LANES]
        for m in extra:
            value = value + got[m, kind, pl.ds(j * 2 * WIDE, 2 * WIDE), :]
        return value

    def tots(kind, extra):
        value = tot[...]
        for m in extra:
            value = value + got[m, kind, pl.ds(ROWS_OUT, 8), :]
        return value

    def deliver(total, m, extra, second, d):
        for kind in (0, 1):
            for e in extra:
                arrived(e, kind)
            for j in (0, 1):
                sent[m, kind, pl.ds(j * 2 * WIDE, 2 * WIDE), :] = piece(total, kind, j, extra)
            sent[m, kind, pl.ds(ROWS_OUT, 8), :] = tots(kind, extra)
            a, b = place(kind)
            if second:
                target = device(kind, step(a, d * sign), b, z)
            else:
                target = device(kind, a, step(b, d * sign), z)
            message(m, kind, target).start()

    for t, d in ((0, 1), (1, -1), (2, 1)):

        def one(u, carry, t=t, d=d):
            deliver(local(t, u), t * 4 + u, [u] if t == 2 else [], False, d)
            return carry

        lax.fori_loop(0, 4, one, 0)

    for u, d in ((0, 1), (1, -1), (2, 1)):
        deliver(local(3, u), 12 + u, [4 + u, 8 + u] + ([12] if u == 2 else []), True, d)

    total = local(3, 3)
    for kind in (0, 1):
        extra = [7, 11, 13, 14]
        for e in extra:
            arrived(e, kind)
        for j in (0, 1):
            value = piece(total, kind, j, extra)
            for n in (0, 1):
                zsent[kind * 4 + j * 2 + n, 0:WIDE, :] = value[n * WIDE : (n + 1) * WIDE, :]
        everything = tots(kind, extra)
        for zh in range(4):
            zsent[kind * 4 + zh, WIDE:PIECE, :] = everything

    def line(d):
        to = (z + d) % NZ
        return remote(
            zsent.at[to], zgot.at[z], zsend_sem.at[to], zrecv_sem.at[z], device(0, y, x, to)
        )

    for d in (4, 3, 5, 2, 6, 1, 7):
        line(d).start()
    summed = zsent[z]
    for d in (1, 7, 2, 6, 3, 5, 4):
        source = (z + d) % NZ
        remote(zsent.at[source], zgot.at[source], zsend_sem.at[source], zrecv_sem.at[source], me).wait_recv()
        summed = summed + zgot[source]

    node = z % 2
    row_ids = lax.broadcasted_iota(jnp.int32, (WIDE, LANES), 0)
    lane_ids = lax.broadcasted_iota(jnp.int32, (WIDE, LANES), 1)
    whole = jnp.broadcast_to(summed[WIDE : WIDE + 1, :], (WIDE, LANES))
    column = jnp.sum(jnp.where(row_ids + node * WIDE == lane_ids, whole, 0.0), axis=1, keepdims=True)
    left_g, left_h = summed[0:TARGETS, :], summed[TARGETS:WIDE, :]
    all_g, all_h = column[0:TARGETS, :], column[TARGETS:WIDE, :]
    right_g, right_h = all_g - left_g, all_h - left_h
    score = (
        left_g * left_g / (left_h + RIDGE)
        + right_g * right_g / (right_h + RIDGE)
        - all_g * all_g / (all_h + RIDGE)
    )
    share[z, 0:TARGETS, :] = -left_g / (left_h + RIDGE)
    share[z, TARGETS:SHARE, :] = jnp.broadcast_to(jnp.sum(score, axis=0, keepdims=True) * (1.0 / TARGETS), (8, LANES))

    def spread_line(slot, to, target):
        return remote(share.at[slot], share.at[slot], ssend_sem.at[to], srecv_sem.at[slot], target)

    for d in (4, 3, 5, 2, 6, 1, 7):
        to = (z + d) % NZ
        spread_line(z, to, device(0, y, x, to)).start()
    for d in (1, 7, 2, 6, 3, 5, 4):
        source = (z + d) % NZ
        spread_line(source, source, me).wait_recv()

    def pass_on(kind, slot, target, k):
        remote(
            pack.at[kind, slot], pack.at[kind, slot], psend_sem.at[kind, k], precv_sem.at[kind, slot], target
        ).start()

    def landed(kind, slot):
        remote(pack.at[kind, slot], pack.at[kind, slot], psend_sem.at[kind, 0], precv_sem.at[kind, slot], me).wait_recv()

    def write(src, kind, b, lanes):
        for a in range(4):
            for j in (0, 1):
                for n in (0, 1):
                    row = n * BINS + kind * 32 + b * 8 + a * 2 + j
                    weights_ref[pl.ds(pl.multiple_of(row * TARGETS, TARGETS), TARGETS), lanes] = src[
                        kind, b * 4 + a, pl.ds((j * 2 + n) * TARGETS, TARGETS), :
                    ]
        for n in (0, 1):
            rows8 = [
                src[kind, b * 4 + a, pl.ds(4 * TARGETS + j * 2 + n, 1), :] for a in range(4) for j in (0, 1)
            ]
            start = pl.multiple_of(n * BINS + kind * 32 + b * 8, 8)
            gains_ref[pl.ds(start, 8), lanes] = jnp.concatenate(rows8, axis=0)

    def to_mate(kind, slot):
        remote(
            pack.at[kind, slot], mate.at[kind, slot], msend_sem.at[kind, slot], mrecv_sem.at[kind, slot], mate_id
        ).start()

    for kind in (0, 1):
        a, b = place(kind)
        slot = b * 4 + a
        for zh in range(4):
            pack[kind, slot, pl.ds(zh * TARGETS, TARGETS), :] = share[kind * 4 + zh, 0:TARGETS, :]
            pack[kind, slot, pl.ds(4 * TARGETS + zh, 1), :] = share[kind * 4 + zh, TARGETS : TARGETS + 1, :]
            pack[kind, slot, pl.ds(4 * TARGETS + 4 + zh, 1), :] = share[kind * 4 + zh, TARGETS : TARGETS + 1, :]
        pass_on(kind, slot, device(kind, step(a, sign), b, z), 0)
        pass_on(kind, slot, device(kind, step(a, -sign), b, z), 1)
        pass_on(kind, slot, device(kind, a, step(b, sign), z), 3)
        pass_on(kind, slot, device(kind, a, step(b, -sign), z), 4)
        to_mate(kind, slot)

    for i, d in ((1, -1), (2, 1), (3, 2)):
        for kind in (0, 1):
            a, b = place(kind)
            slot = b * 4 + step(a, d * sign)
            landed(kind, slot)
            if i == 1:
                pass_on(kind, slot, device(kind, step(a, sign), b, z), 2)
            pass_on(kind, slot, device(kind, a, step(b, sign), z), 3 + 2 * i)
            pass_on(kind, slot, device(kind, a, step(b, -sign), z), 4 + 2 * i)
            to_mate(kind, slot)

    for d2 in (-1, 1, 2):
        for i, d in ((0, 0), (1, -1), (2, 1), (3, 2)):
            for kind in (0, 1):
                a, b = place(kind)
                slot = step(b, d2 * sign) * 4 + step(a, d * sign)
                landed(kind, slot)
                if d2 == -1:
                    pass_on(kind, slot, device(kind, a, step(b, sign), z), 11 + i)
                to_mate(kind, slot)

    def finish(b, carry):
        for kind in (0, 1):
            write(pack, kind, b, own_lanes)
        return carry

    lax.fori_loop(0, 4, finish, 0)

    def finish_mate(b, carry):
        for kind in (0, 1):
            for a in range(4):
                slot = b * 4 + a
                remote(
                    mate.at[kind, slot], mate.at[kind, slot], msend_sem.at[kind, slot], mrecv_sem.at[kind, slot], me
                ).wait_recv()
            write(mate, kind, b, mate_lanes)
        return carry

    lax.fori_loop(0, 4, finish_mate, 0)

    pair_bins.wait_send()
    pair_vals.wait_send()

    def drain(m, carry):
        for kind in (0, 1):
            message(m, kind, me).wait_send()
            remote(pack.at[kind, 0], pack.at[kind, 0], psend_sem.at[kind, m], precv_sem.at[kind, 0], me).wait_send()
        return carry

    lax.fori_loop(0, 15, drain, 0)

    def drain_mate(slot, carry):
        for kind in (0, 1):
            remote(
                pack.at[kind, slot], pack.at[kind, slot], msend_sem.at[kind, slot], mrecv_sem.at[kind, slot], me
            ).wait_send()
        return carry

    lax.fori_loop(0, PLANE, drain_mate, 0)
    for d in range(1, NZ):
        to = (z + d) % NZ
        line(d).wait_send()
        spread_line(z, to, me).wait_send()


def on_device(bin_index, node_ids, gradients, hessians):
    rows, features = bin_index.shape
    dma = pltpu.SemaphoreType.DMA
    f32 = jnp.float32
    whole = pl.BlockSpec(memory_space=pltpu.VMEM)
    weights, gains = pl.pallas_call(
        functools.partial(kernel, rows),
        out_shape=(
            jax.ShapeDtypeStruct((2 * BINS * TARGETS, features), f32),
            jax.ShapeDtypeStruct((2 * BINS, features), f32),
        ),
        in_specs=[pl.BlockSpec(memory_space=pl.ANY), whole, whole, whole],
        out_specs=(whole, whole),
        scratch_shapes=[
            pltpu.VMEM((2 * rows, LANES), jnp.int32),
            pltpu.VMEM((2 * WIDE, 2 * rows), jnp.bfloat16),
            pltpu.VMEM((PIECE, rows), f32),
            pltpu.VMEM((PIECE, rows), f32),
            pltpu.VMEM((8, LANES), f32),
            pltpu.VMEM((15, 2, MESSAGE, LANES), f32),
            pltpu.VMEM((15, 2, MESSAGE, LANES), f32),
            pltpu.VMEM((NZ, PIECE, LANES), f32),
            pltpu.VMEM((NZ, PIECE, LANES), f32),
            pltpu.VMEM((NZ, SHARE, LANES), f32),
            pltpu.VMEM((2, PLANE, PACK, LANES), f32),
            pltpu.VMEM((2, PLANE, PACK, LANES), f32),
            dma((1,)),
            dma((2,)),
            dma((2,)),
            dma((15, 2)),
            dma((15, 2)),
            dma((NZ,)),
            dma((NZ,)),
            dma((NZ,)),
            dma((NZ,)),
            dma((2, 15)),
            dma((2, PLANE)),
            dma((2, PLANE)),
            dma((2, PLANE)),
        ],
        compiler_params=pltpu.CompilerParams(collective_id=0, has_side_effects=True, vmem_limit_bytes=56 << 20),
        name="level",
    )(bin_index, node_ids.reshape(1, rows), gradients.T, hessians.T)
    weights = jnp.transpose(weights.reshape(2, BINS, TARGETS, features), (3, 0, 1, 2))
    gains = jnp.transpose(gains.reshape(2, BINS, features), (2, 0, 1))
    return (gains, weights)


def solution(mesh):
    return jax.shard_map(
        on_device,
        mesh=mesh,
        in_specs=(P("dp", None), P("dp"), P("dp", None), P("dp", None)),
        out_specs=(P(), P()),
        check_vma=False,
    )
```

```python
import functools

import jax
import jax.numpy as jnp
from jax import lax
from jax.experimental import pallas as pl
from jax.experimental.pallas import tpu as pltpu
from jax.sharding import PartitionSpec as P

MESH = pl.DeviceIdType.MESH

BINS = 64
TARGETS = 32
WIDE = 2 * TARGETS
LANES = 128
NX, NY, NZ = 4, 4, 8
PLANE = NX * NY
RIDGE = 1.0
DEPTH = 1024
PIECE = WIDE + 8
EARLY = 3
LAG = 3
SHARE = TARGETS + 8
PACK = 4 * TARGETS + 8


def offset(u):
    high, low = u // 2, u % 2
    return (2 + low) * (1 - high) + (1 - low) * high


def kernel(
    rows,
    bins_hbm,
    node_hbm,
    grad_hbm,
    hess_hbm,
    weights_ref,
    gains_ref,
    node_ref,
    grad_ref,
    hess_ref,
    bins,
    spread,
    mine,
    theirs,
    early,
    tz,
    tline,
    raw,
    pairs,
    paired,
    sent1,
    got1,
    sent0,
    got0,
    zsent,
    zgot,
    share,
    pack,
    mate,
    own_sem,
    swap_send,
    swap_recv,
    tz_send,
    tz_recv,
    tl_send,
    tl_recv,
    pair_send,
    pair_recv,
    send1,
    recv1,
    send0,
    recv0,
    zsend,
    zrecv,
    ssend_sem,
    srecv_sem,
    psend_sem,
    precv_sem,
    msend_sem,
    mrecv_sem,
):
    me = lax.axis_index("dp")
    core = me % 2
    z = (me // 2) % NZ
    y = (me // (2 * NZ)) % NY
    x = me // (2 * NZ * NY)
    sign = 1 - 2 * core
    other = 1 - core
    mate_id = me + sign
    h = z % 2
    partners = ((z + 1 - 2 * h + NZ) % NZ, (z - 1 + 2 * h + NZ) % NZ)

    def device(kind, a, b, zz):
        xx, yy = (b, a) if kind == 0 else (a, b)
        return ((xx * NY + yy) * NZ + zz) * 2 + core

    def place(kind):
        return (y, x) if kind == 0 else (x, y)

    def step(p, d):
        return (p + d + 8) % 4

    def remote(src, dst, send, recv, target):
        return pltpu.make_async_remote_copy(
            src_ref=src, dst_ref=dst, send_sem=send, recv_sem=recv, device_id=(target,), device_id_type=MESH
        )

    own_lanes = pl.ds(pl.multiple_of(core * LANES, LANES), LANES)
    mate_lanes = pl.ds(pl.multiple_of(other * LANES, LANES), LANES)
    loads = [
        pltpu.make_async_copy(grad_hbm, grad_ref, own_sem.at[0]),
        pltpu.make_async_copy(hess_hbm, hess_ref, own_sem.at[1]),
        pltpu.make_async_copy(node_hbm, node_ref, own_sem.at[2]),
        pltpu.make_async_copy(bins_hbm.at[:, own_lanes], bins.at[pl.ds(0, rows)], own_sem.at[3]),
    ]
    for load in loads:
        load.start()

    barrier = pltpu.get_barrier_semaphore()
    greeted = [mate_id]
    for kind in (0, 1):
        a, b = place(kind)
        greeted += [device(kind, a, step(b, d), z) for d in (1, 2, 3)]
    for d in range(1, NZ):
        greeted.append(device(0, y, x, (z + d) % NZ))
    for peer in greeted:
        pl.semaphore_signal(barrier, inc=1, device_id=(peer,), device_id_type=MESH)

    for load in loads[:3]:
        load.wait()
    mine[0:TARGETS, :] = grad_ref[...].astype(jnp.float32)
    mine[TARGETS:WIDE, :] = hess_ref[...].astype(jnp.float32)
    mine[WIDE:PIECE, :] = jnp.broadcast_to(node_ref[...].astype(jnp.float32), (8, rows))

    pl.semaphore_wait(barrier, len(greeted))

    swap_vals = remote(mine, theirs, swap_send.at[1], swap_recv.at[1], mate_id)
    swap_bins = remote(bins_hbm.at[:, mate_lanes], bins.at[pl.ds(rows, rows)], swap_send.at[0], swap_recv.at[0], mate_id)
    swap_vals.start()
    swap_bins.start()

    def fill(values, start):
        which = values[WIDE : WIDE + 1, :]
        both = values[0:WIDE, :]
        for n in (0, 1):
            part = jnp.where(which == float(n), both, 0.0)
            spread[n * WIDE : (n + 1) * WIDE, start : start + rows] = part.astype(jnp.bfloat16)

    def local(i, low, high):
        t, u = i // 4, i % 4
        firsts = []
        for kind in (0, 1):
            a, b = place(kind)
            firsts.append(kind * 32 + step(b, offset(t) * sign) * 8 + step(a, offset(u) * sign) * 2)
        total = None
        for start in range(low, high, DEPTH):
            block = bins[start : start + DEPTH, :]
            hot = [
                jnp.where(block <= first + j, jnp.ones((), jnp.bfloat16), jnp.zeros((), jnp.bfloat16))
                for first in firsts
                for j in (0, 1)
            ]
            term = jnp.dot(
                spread[:, start : start + DEPTH], jnp.concatenate(hot, axis=1), preferred_element_type=jnp.float32
            )
            total = term if total is None else total + term
        return total

    def tz_copy(slot, target):
        return remote(tz.at[slot], tz.at[slot], tz_send.at[target], tz_recv.at[slot], device(0, y, x, target))

    def tl_copy(kind, slot, to):
        a, b = place(kind)
        return remote(
            tline.at[kind, slot], tline.at[kind, slot], tl_send.at[kind, to], tl_recv.at[kind, slot], device(kind, a, to, z)
        )

    def totals_begin():
        ones = jnp.ones((8, 2 * rows), jnp.bfloat16)
        tz[z] = lax.dot_general(ones, spread[...], (((1,), (1,)), ((), ())), preferred_element_type=jnp.float32)
        for d in range(1, NZ):
            tz_copy(z, (z + d) % NZ).start()

    def totals_z():
        value = tz[z]
        for d in range(1, NZ):
            source = (z + d) % NZ
            tz_copy(source, source).wait_recv()
            value = value + tz[source]
        return value

    def totals_line(kind):
        a, b = place(kind)
        value = tline[kind, b]
        for d in (1, 2, 3):
            source = step(b, d)
            tl_copy(kind, source, source).wait_recv()
            value = value + tline[kind, source]
        return value

    def totals_send(kind, value):
        a, b = place(kind)
        tline[kind, b] = value
        for d in (1, 2, 3):
            tl_copy(kind, b, step(b, d)).start()

    def one(m, kind, target):
        return remote(sent1.at[m, kind], got1.at[m, kind], send1.at[m, kind], recv1.at[m, kind], target)

    def zero(m, kind, target):
        return remote(sent0.at[m, kind], got0.at[m, kind], send0.at[m, kind], recv0.at[m, kind], target)

    def pair(i, kind):
        a, b = place(kind)
        return remote(
            pairs.at[i, kind, 1 - h],
            paired.at[i, kind],
            pair_send.at[i, kind],
            pair_recv.at[i, kind],
            device(kind, a, b, partners[kind]),
        )

    toward = (1, -1, 1)

    def extras(i):
        t, u = i // 4, i % 4
        if t < 2:
            return []
        if t == 2:
            return [u]
        return [4 + u, 8 + u] + ([12] if u == 2 else []) + ([13, 14] if u == 3 else [])

    def target_of(i, kind):
        t, u = i // 4, i % 4
        a, b = place(kind)
        if t < 3:
            return device(kind, a, step(b, toward[t] * sign), z)
        return device(kind, step(a, toward[u] * sign), b, z)

    def put1(i, kind, value):
        for e in extras(i):
            one(e, kind, me).wait_recv()
            value = value + got1[e, kind]
        if i == 15:
            for n in (0, 1):
                zsent[kind * 4 + 2 + n] = value[n * WIDE : (n + 1) * WIDE, :]
        else:
            sent1[i, kind] = value
            one(i, kind, target_of(i, kind)).start()

    def put0(i):
        for kind in (0, 1):
            pair(i, kind).wait_recv()
            value = pairs[i, kind, h] + paired[i, kind]
            for e in extras(i):
                zero(e, kind, me).wait_recv()
                value = value + got0[e, kind]
            if i == 15:
                zsent[kind * 4 + h] = value
            else:
                sent0[i, kind] = value
                zero(i, kind, target_of(i, kind)).start()

    def late1(i):
        for kind in (0, 1):
            put1(i, kind, raw[i - 12, kind])

    def take(i, total):
        for kind in (0, 1):
            first = total[:, 2 * kind * LANES : (2 * kind + 1) * LANES]
            pairs[i, kind, 0] = first[0:WIDE, :]
            pairs[i, kind, 1] = first[WIDE : 2 * WIDE, :]
            pair(i, kind).start()
            second = total[:, (2 * kind + 1) * LANES : (2 * kind + 2) * LANES]
            if i < 12:
                put1(i, kind, second)
            else:
                raw[i - 12, kind] = second

    fill(mine, 0)
    loads[3].wait()
    for i in range(EARLY):
        early[i] = local(i, 0, rows)
    swap_vals.wait_recv()
    fill(theirs, rows)
    swap_bins.wait_recv()

    for i in range(16):
        if i < EARLY:
            take(i, early[i] + local(i, rows, 2 * rows))
        else:
            take(i, local(i, 0, 2 * rows))
        if i == 1:
            totals_begin()
        if i == 5:
            totals_send(0, totals_z())
        if i == 9:
            totals_send(1, totals_line(0))
        if LAG <= i:
            if i - LAG < 12:
                put0(i - LAG)
        if i == 13:
            late1(12)
        if i == 14:
            late1(13)
    put0(12)
    late1(14)
    put0(13)
    put0(14)
    late1(15)

    def line(to):
        return remote(zsent.at[to], zgot.at[z], zsend.at[to], zrecv.at[z], device(0, y, x, to))

    def wide(zz):
        return (zz // 2) % 2 == 1

    for d in (4, 3, 5, 2, 6, 1, 7):
        to = (z + d) % NZ

        @pl.when(wide(to))
        def _(to=to):
            line(to).start()

    put0(15)
    for d in (4, 2, 6):
        to = (z + d) % NZ

        @pl.when(jnp.logical_not(wide(to)))
        def _(to=to):
            line(to).start()

    everything = totals_line(1)

    def come(d):
        source = (z + d) % NZ
        remote(zsent.at[source], zgot.at[source], zsend.at[source], zrecv.at[source], me).wait_recv()
        return zgot[source]

    @pl.when(wide(z))
    def _():
        value = zsent[z]
        for d in (1, 7, 3, 5):
            value = value + come(d)
        zsent[z] = value

    summed = zsent[z]
    for d in (2, 6, 4):
        summed = summed + come(d)

    row_ids = lax.broadcasted_iota(jnp.int32, (WIDE, LANES), 0)
    lane_ids = lax.broadcasted_iota(jnp.int32, (WIDE, LANES), 1)
    whole = jnp.broadcast_to(everything[0:1, :], (WIDE, LANES))
    column = jnp.sum(jnp.where(row_ids + h * WIDE == lane_ids, whole, 0.0), axis=1, keepdims=True)
    left_g, left_h = summed[0:TARGETS, :], summed[TARGETS:WIDE, :]
    all_g, all_h = column[0:TARGETS, :], column[TARGETS:WIDE, :]
    right_g, right_h = all_g - left_g, all_h - left_h
    score = (
        left_g * left_g / (left_h + RIDGE)
        + right_g * right_g / (right_h + RIDGE)
        - all_g * all_g / (all_h + RIDGE)
    )
    share[z, 0:TARGETS, :] = -left_g / (left_h + RIDGE)
    share[z, TARGETS:SHARE, :] = jnp.broadcast_to(jnp.sum(score, axis=0, keepdims=True) * (1.0 / TARGETS), (8, LANES))

    def spread_line(slot, to, target):
        return remote(share.at[slot], share.at[slot], ssend_sem.at[to], srecv_sem.at[slot], target)

    for d in (4, 3, 5, 2, 6, 1, 7):
        to = (z + d) % NZ
        spread_line(z, to, device(0, y, x, to)).start()
    for d in (1, 7, 2, 6, 3, 5, 4):
        source = (z + d) % NZ
        spread_line(source, source, me).wait_recv()

    def pass_on(kind, slot, target, k):
        remote(
            pack.at[kind, slot], pack.at[kind, slot], psend_sem.at[kind, k], precv_sem.at[kind, slot], target
        ).start()

    def landed(kind, slot):
        remote(pack.at[kind, slot], pack.at[kind, slot], psend_sem.at[kind, 0], precv_sem.at[kind, slot], me).wait_recv()

    def write(src, kind, b, lanes):
        for a in range(4):
            for j in (0, 1):
                for n in (0, 1):
                    row = n * BINS + kind * 32 + b * 8 + a * 2 + j
                    weights_ref[pl.ds(pl.multiple_of(row * TARGETS, TARGETS), TARGETS), lanes] = src[
                        kind, b * 4 + a, pl.ds((j * 2 + n) * TARGETS, TARGETS), :
                    ]
        for n in (0, 1):
            rows8 = [
                src[kind, b * 4 + a, pl.ds(4 * TARGETS + j * 2 + n, 1), :] for a in range(4) for j in (0, 1)
            ]
            start = pl.multiple_of(n * BINS + kind * 32 + b * 8, 8)
            gains_ref[pl.ds(start, 8), lanes] = jnp.concatenate(rows8, axis=0)

    def to_mate(kind, slot):
        remote(
            pack.at[kind, slot], mate.at[kind, slot], msend_sem.at[kind, slot], mrecv_sem.at[kind, slot], mate_id
        ).start()

    ways = (0, -1, 1, 2)

    def at(kind, i, k):
        a, b = place(kind)
        return step(b, ways[k] * sign) * 4 + step(a, ways[i] * sign)

    for kind in (0, 1):
        a, b = place(kind)
        slot = b * 4 + a
        for zh in range(4):
            pack[kind, slot, pl.ds(zh * TARGETS, TARGETS), :] = share[kind * 4 + zh, 0:TARGETS, :]
            pack[kind, slot, pl.ds(4 * TARGETS + zh, 1), :] = share[kind * 4 + zh, TARGETS : TARGETS + 1, :]
            pack[kind, slot, pl.ds(4 * TARGETS + 4 + zh, 1), :] = share[kind * 4 + zh, TARGETS : TARGETS + 1, :]
        pass_on(kind, slot, device(kind, step(a, 2), b, z), 2)
        pass_on(kind, slot, device(kind, step(a, sign), b, z), 0)
        pass_on(kind, slot, device(kind, step(a, -sign), b, z), 1)

    def across(kind, i):
        a, b = place(kind)
        slot = at(kind, i, 0)
        if i == 3:
            pass_on(kind, slot, device(kind, a, step(b, 2), z), 14)
        pass_on(kind, slot, device(kind, a, step(b, sign), z), 3 + 2 * i)
        pass_on(kind, slot, device(kind, a, step(b, -sign), z), 4 + 2 * i)
        to_mate(kind, slot)

    def onward(i):
        for kind in (0, 1):
            landed(kind, at(kind, i, 1))
            a, b = place(kind)
            pass_on(kind, at(kind, i, 1), device(kind, a, step(b, sign), z), 11 + i)
            to_mate(kind, at(kind, i, 1))

    for kind in (0, 1):
        across(kind, 0)
    for i in (1, 2, 3):
        for kind in (0, 1):
            landed(kind, at(kind, i, 0))
            across(kind, i)
        if i == 2:
            onward(0)
    onward(1)
    onward(2)
    for i, k in ((0, 2), (0, 3), (1, 2), (2, 2), (3, 1), (3, 2), (1, 3), (2, 3), (3, 3)):
        for kind in (0, 1):
            landed(kind, at(kind, i, k))
            to_mate(kind, at(kind, i, k))

    def finish(b, carry):
        for kind in (0, 1):
            write(pack, kind, b, own_lanes)
        return carry

    lax.fori_loop(0, 4, finish, 0)

    def finish_mate(b, carry):
        for kind in (0, 1):
            for a in range(4):
                slot = b * 4 + a
                remote(
                    mate.at[kind, slot], mate.at[kind, slot], msend_sem.at[kind, slot], mrecv_sem.at[kind, slot], me
                ).wait_recv()
            write(mate, kind, b, mate_lanes)
        return carry

    lax.fori_loop(0, 4, finish_mate, 0)

    swap_bins.wait_send()
    swap_vals.wait_send()
    for kind in (0, 1):
        a, b = place(kind)
        for d in (1, 2, 3):
            tl_copy(kind, b, step(b, d)).wait_send()
    for d in range(1, NZ):
        to = (z + d) % NZ
        tz_copy(z, to).wait_send()
        spread_line(z, to, me).wait_send()
        if d % 2 == 0:
            line(to).wait_send()
        else:

            @pl.when(wide(to))
            def _(to=to):
                line(to).wait_send()

    def drain(m, carry):
        for kind in (0, 1):
            one(m, kind, me).wait_send()
            zero(m, kind, me).wait_send()
            remote(pack.at[kind, 0], pack.at[kind, 0], psend_sem.at[kind, m], precv_sem.at[kind, 0], me).wait_send()
        return carry

    lax.fori_loop(0, 15, drain, 0)

    def drain_pairs(m, carry):
        for kind in (0, 1):
            pair(m, kind).wait_send()
            remote(
                pack.at[kind, m], pack.at[kind, m], msend_sem.at[kind, m], mrecv_sem.at[kind, m], me
            ).wait_send()
        return carry

    lax.fori_loop(0, PLANE, drain_pairs, 0)


def on_device(bin_index, node_ids, gradients, hessians):
    rows, features = bin_index.shape
    dma = pltpu.SemaphoreType.DMA
    vmem = pltpu.VMEM
    f32 = jnp.float32
    whole = pl.BlockSpec(memory_space=pltpu.VMEM)
    operands = [bin_index, node_ids.reshape(1, rows), gradients.T, hessians.T]
    weights, gains = pl.pallas_call(
        functools.partial(kernel, rows),
        out_shape=(
            jax.ShapeDtypeStruct((2 * BINS * TARGETS, features), f32),
            jax.ShapeDtypeStruct((2 * BINS, features), f32),
        ),
        in_specs=[pl.BlockSpec(memory_space=pltpu.HBM)] * 4,
        out_specs=(whole, whole),
        scratch_shapes=[
            vmem((1, rows), jnp.int32),
            vmem((TARGETS, rows), jnp.bfloat16),
            vmem((TARGETS, rows), jnp.bfloat16),
            vmem((2 * rows, LANES), jnp.int32),
            vmem((2 * WIDE, 2 * rows), jnp.bfloat16),
            vmem((PIECE, rows), f32),
            vmem((PIECE, rows), f32),
            vmem((EARLY, 2 * WIDE, 4 * LANES), f32),
            vmem((NZ, 8, LANES), f32),
            vmem((2, 4, 8, LANES), f32),
            vmem((4, 2, 2 * WIDE, LANES), f32),
            vmem((16, 2, 2, WIDE, LANES), f32),
            vmem((16, 2, WIDE, LANES), f32),
            vmem((15, 2, 2 * WIDE, LANES), f32),
            vmem((15, 2, 2 * WIDE, LANES), f32),
            vmem((15, 2, WIDE, LANES), f32),
            vmem((15, 2, WIDE, LANES), f32),
            vmem((NZ, WIDE, LANES), f32),
            vmem((NZ, WIDE, LANES), f32),
            vmem((NZ, SHARE, LANES), f32),
            vmem((2, PLANE, PACK, LANES), f32),
            vmem((2, PLANE, PACK, LANES), f32),
            dma((4,)),
            dma((2,)),
            dma((2,)),
            dma((NZ,)),
            dma((NZ,)),
            dma((2, 4)),
            dma((2, 4)),
            dma((16, 2)),
            dma((16, 2)),
            dma((15, 2)),
            dma((15, 2)),
            dma((15, 2)),
            dma((15, 2)),
            dma((NZ,)),
            dma((NZ,)),
            dma((NZ,)),
            dma((NZ,)),
            dma((2, 15)),
            dma((2, PLANE)),
            dma((2, PLANE)),
            dma((2, PLANE)),
        ],
        compiler_params=pltpu.CompilerParams(collective_id=0, has_side_effects=True, vmem_limit_bytes=30 << 20),
        name="level",
    )(*[pltpu.with_memory_space_constraint(v, pltpu.HBM) for v in operands])
    weights = jnp.transpose(weights.reshape(2, BINS, TARGETS, features), (3, 0, 1, 2))
    gains = jnp.transpose(gains.reshape(2, BINS, features), (2, 0, 1))
    return (gains, weights)


def solution(mesh):
    return jax.shard_map(
        on_device,
        mesh=mesh,
        in_specs=(P("dp", None), P("dp"), P("dp", None), P("dp", None)),
        out_specs=(P(), P()),
        check_vma=False,
    )
```

```python
import functools

import jax
import jax.numpy as jnp
from jax import lax
from jax.experimental import pallas as pl
from jax.experimental.pallas import tpu as pltpu
from jax.sharding import PartitionSpec as P

MESH = pl.DeviceIdType.MESH

BINS = 64
TARGETS = 32
WIDE = 2 * TARGETS
LANES = 128
NX, NY, NZ = 4, 4, 8
PLANE = NX * NY
RIDGE = 1.0
DEPTH = 1024
PIECE = WIDE + 8
EARLY = 4
SHARE = TARGETS + 8
PACK = 4 * TARGETS + 8


def offset(u):
    high, low = u // 2, u % 2
    return (2 + low) * (1 - high) + (1 - low) * high


def kernel(
    rows,
    bins_hbm,
    node_hbm,
    grad_hbm,
    hess_hbm,
    weights_ref,
    gains_ref,
    node_ref,
    grad_ref,
    hess_ref,
    bins,
    spread,
    mine,
    theirs,
    early,
    tz,
    tline,
    raw,
    pairs,
    paired,
    sent1,
    got1,
    sent0,
    got0,
    zsent,
    zgot,
    share,
    pack,
    mate,
    own_sem,
    swap_send,
    swap_recv,
    tz_send,
    tz_recv,
    tl_send,
    tl_recv,
    pair_send,
    pair_recv,
    send1,
    recv1,
    send0,
    recv0,
    zsend,
    zrecv,
    ssend_sem,
    srecv_sem,
    psend_sem,
    precv_sem,
    msend_sem,
    mrecv_sem,
):
    me = lax.axis_index("dp")
    core = me % 2
    z = (me // 2) % NZ
    y = (me // (2 * NZ)) % NY
    x = me // (2 * NZ * NY)
    sign = 1 - 2 * core
    other = 1 - core
    mate_id = me + sign
    h = z % 2
    partners = ((z + 1 - 2 * h + NZ) % NZ, (z - 1 + 2 * h + NZ) % NZ)

    def device(kind, a, b, zz):
        xx, yy = (b, a) if kind == 0 else (a, b)
        return ((xx * NY + yy) * NZ + zz) * 2 + core

    def place(kind):
        return (y, x) if kind == 0 else (x, y)

    def step(p, d):
        return (p + d + 8) % 4

    def remote(src, dst, send, recv, target):
        return pltpu.make_async_remote_copy(
            src_ref=src, dst_ref=dst, send_sem=send, recv_sem=recv, device_id=(target,), device_id_type=MESH
        )

    own_lanes = pl.ds(pl.multiple_of(core * LANES, LANES), LANES)
    mate_lanes = pl.ds(pl.multiple_of(other * LANES, LANES), LANES)
    loads = [
        pltpu.make_async_copy(grad_hbm, grad_ref, own_sem.at[0]),
        pltpu.make_async_copy(hess_hbm, hess_ref, own_sem.at[1]),
        pltpu.make_async_copy(node_hbm, node_ref, own_sem.at[2]),
        pltpu.make_async_copy(bins_hbm.at[:, own_lanes], bins.at[pl.ds(0, rows)], own_sem.at[3]),
    ]
    for load in loads:
        load.start()

    barrier = pltpu.get_barrier_semaphore()
    greeted = [mate_id]
    for kind in (0, 1):
        a, b = place(kind)
        greeted += [device(kind, a, step(b, d), z) for d in (1, 2, 3)]
    for d in range(1, NZ):
        greeted.append(device(0, y, x, (z + d) % NZ))
    for peer in greeted:
        pl.semaphore_signal(barrier, inc=1, device_id=(peer,), device_id_type=MESH)

    for load in loads[:3]:
        load.wait()
    mine[0:TARGETS, :] = grad_ref[...].astype(jnp.float32)
    mine[TARGETS:WIDE, :] = hess_ref[...].astype(jnp.float32)
    mine[WIDE:PIECE, :] = jnp.broadcast_to(node_ref[...].astype(jnp.float32), (8, rows))

    pl.semaphore_wait(barrier, len(greeted))

    swap_vals = remote(mine, theirs, swap_send.at[1], swap_recv.at[1], mate_id)
    swap_bins = remote(bins_hbm.at[:, mate_lanes], bins.at[pl.ds(rows, rows)], swap_send.at[0], swap_recv.at[0], mate_id)
    swap_vals.start()
    swap_bins.start()

    def fill(values, start):
        which = values[WIDE : WIDE + 1, :]
        both = values[0:WIDE, :]
        for n in (0, 1):
            part = jnp.where(which == float(n), both, 0.0)
            spread[n * WIDE : (n + 1) * WIDE, start : start + rows] = part.astype(jnp.bfloat16)

    def local(t, u, low, high):
        firsts = []
        for kind in (0, 1):
            a, b = place(kind)
            firsts.append(kind * 32 + step(b, offset(t) * sign) * 8 + step(a, offset(u) * sign) * 2)
        total = None
        for start in range(low, high, DEPTH):
            block = bins[start : start + DEPTH, :]
            hot = [
                jnp.where(block <= first + j, jnp.ones((), jnp.bfloat16), jnp.zeros((), jnp.bfloat16))
                for first in firsts
                for j in (0, 1)
            ]
            term = jnp.dot(
                spread[:, start : start + DEPTH], jnp.concatenate(hot, axis=1), preferred_element_type=jnp.float32
            )
            total = term if total is None else total + term
        return total

    def tz_copy(slot, target):
        return remote(tz.at[slot], tz.at[slot], tz_send.at[target], tz_recv.at[slot], device(0, y, x, target))

    def tl_copy(kind, slot, to):
        a, b = place(kind)
        return remote(
            tline.at[kind, slot], tline.at[kind, slot], tl_send.at[kind, to], tl_recv.at[kind, slot], device(kind, a, to, z)
        )

    def totals_begin():
        ones = jnp.ones((8, 2 * rows), jnp.bfloat16)
        tz[z] = lax.dot_general(ones, spread[...], (((1,), (1,)), ((), ())), preferred_element_type=jnp.float32)
        for d in range(1, NZ):
            tz_copy(z, (z + d) % NZ).start()

    def totals_z():
        value = tz[z]
        for d in range(1, NZ):
            source = (z + d) % NZ
            tz_copy(source, source).wait_recv()
            value = value + tz[source]
        return value

    def totals_line(kind):
        a, b = place(kind)
        value = tline[kind, b]
        for d in (1, 2, 3):
            source = step(b, d)
            tl_copy(kind, source, source).wait_recv()
            value = value + tline[kind, source]
        return value

    def totals_send(kind, value):
        a, b = place(kind)
        tline[kind, b] = value
        for d in (1, 2, 3):
            tl_copy(kind, b, step(b, d)).start()

    def one(m, kind, target):
        return remote(sent1.at[m, kind], got1.at[m, kind], send1.at[m, kind], recv1.at[m, kind], target)

    def zero(m, kind, target):
        return remote(sent0.at[m, kind], got0.at[m, kind], send0.at[m, kind], recv0.at[m, kind], target)

    def pair(i, kind):
        a, b = place(kind)
        return remote(
            pairs.at[i, kind, 1 - h],
            paired.at[i, kind],
            pair_send.at[i, kind],
            pair_recv.at[i, kind],
            device(kind, a, b, partners[kind]),
        )

    toward = (1, -1, 1)

    def extras(t, u):
        if t < 2:
            return []
        if t == 2:
            return [u]
        return [4 + u, 8 + u] + {2: [12], 3: [13, 14]}.get(u, [])

    def target_of(t, u, kind):
        a, b = place(kind)
        if t < 3:
            return device(kind, a, step(b, toward[t] * sign), z)
        return device(kind, step(a, toward[u] * sign), b, z)

    def put1(t, u, kind, value):
        i = t * 4 + u
        last = t == 3 and u == 3
        for e in extras(t, u):
            one(e, kind, me).wait_recv()
            value = value + got1[e, kind]
        if last:
            for n in (0, 1):
                zsent[kind * 4 + 2 + n] = value[n * WIDE : (n + 1) * WIDE, :]
        else:
            sent1[i, kind] = value
            one(i, kind, target_of(t, u, kind)).start()

    def put0(t, u):
        i = t * 4 + u
        last = t == 3 and u == 3
        for kind in (0, 1):
            pair(i, kind).wait_recv()
            value = pairs[i, kind, h] + paired[i, kind]
            for e in extras(t, u):
                zero(e, kind, me).wait_recv()
                value = value + got0[e, kind]
            if last:
                zsent[kind * 4 + h] = value
            else:
                sent0[i, kind] = value
                zero(i, kind, target_of(t, u, kind)).start()

    def late1(u):
        for kind in (0, 1):
            put1(3, u, kind, raw[u, kind])

    def take(t, u, total):
        i = t * 4 + u
        for kind in (0, 1):
            first = total[:, 2 * kind * LANES : (2 * kind + 1) * LANES]
            pairs[i, kind, 0] = first[0:WIDE, :]
            pairs[i, kind, 1] = first[WIDE : 2 * WIDE, :]
            pair(i, kind).start()
            second = total[:, (2 * kind + 1) * LANES : (2 * kind + 2) * LANES]
            if t < 3:
                put1(t, u, kind, second)
            else:
                raw[u, kind] = second

    fill(mine, 0)
    loads[3].wait()
    def begin(u, carry):
        early[u] = local(0, u, 0, rows)
        return carry

    lax.fori_loop(0, EARLY, begin, 0)
    swap_vals.wait_recv()
    fill(theirs, rows)
    swap_bins.wait_recv()

    for t in range(4):

        def stage(u, carry, t=t):
            if t == 0:
                take(0, u, early[u] + local(0, u, rows, 2 * rows))
            else:
                take(t, u, local(t, u, 0, 2 * rows))
                put0(t - 1, u)
            return carry

        lax.fori_loop(0, 3 if t == 3 else 4, stage, 0)
        if t == 0:
            totals_begin()
        if t == 2:
            totals_send(0, totals_z())

    late1(0)
    take(3, 3, local(3, 3, 0, 2 * rows))
    late1(1)
    put0(2, 3)
    put0(3, 0)
    late1(2)
    put0(3, 1)
    totals_send(1, totals_line(0))
    put0(3, 2)
    late1(3)

    def line(to):
        return remote(zsent.at[to], zgot.at[z], zsend.at[to], zrecv.at[z], device(0, y, x, to))

    def wide(zz):
        return (zz // 2) % 2 == 1

    for d in (4, 3, 5, 2, 6, 1, 7):
        to = (z + d) % NZ

        @pl.when(wide(to))
        def _(to=to):
            line(to).start()

    put0(3, 3)
    for d in (4, 2, 6):
        to = (z + d) % NZ

        @pl.when(jnp.logical_not(wide(to)))
        def _(to=to):
            line(to).start()

    everything = totals_line(1)

    def come(d):
        source = (z + d) % NZ
        remote(zsent.at[source], zgot.at[source], zsend.at[source], zrecv.at[source], me).wait_recv()
        return zgot[source]

    @pl.when(wide(z))
    def _():
        value = zsent[z]
        for d in (1, 7, 3, 5):
            value = value + come(d)
        zsent[z] = value

    summed = zsent[z]
    for d in (2, 6, 4):
        summed = summed + come(d)

    row_ids = lax.broadcasted_iota(jnp.int32, (WIDE, LANES), 0)
    lane_ids = lax.broadcasted_iota(jnp.int32, (WIDE, LANES), 1)
    whole = jnp.broadcast_to(everything[0:1, :], (WIDE, LANES))
    column = jnp.sum(jnp.where(row_ids + h * WIDE == lane_ids, whole, 0.0), axis=1, keepdims=True)
    left_g, left_h = summed[0:TARGETS, :], summed[TARGETS:WIDE, :]
    all_g, all_h = column[0:TARGETS, :], column[TARGETS:WIDE, :]
    right_g, right_h = all_g - left_g, all_h - left_h
    score = (
        left_g * left_g / (left_h + RIDGE)
        + right_g * right_g / (right_h + RIDGE)
        - all_g * all_g / (all_h + RIDGE)
    )
    share[z, 0:TARGETS, :] = -left_g / (left_h + RIDGE)
    share[z, TARGETS:SHARE, :] = jnp.broadcast_to(jnp.sum(score, axis=0, keepdims=True) * (1.0 / TARGETS), (8, LANES))

    def spread_line(slot, to, target):
        return remote(share.at[slot], share.at[slot], ssend_sem.at[to], srecv_sem.at[slot], target)

    for d in (4, 3, 5, 2, 6, 1, 7):
        to = (z + d) % NZ
        spread_line(z, to, device(0, y, x, to)).start()
    for d in (1, 7, 2, 6, 3, 5, 4):
        source = (z + d) % NZ
        spread_line(source, source, me).wait_recv()

    def pass_on(kind, slot, target, k):
        remote(
            pack.at[kind, slot], pack.at[kind, slot], psend_sem.at[kind, k], precv_sem.at[kind, slot], target
        ).start()

    def landed(kind, slot):
        remote(pack.at[kind, slot], pack.at[kind, slot], psend_sem.at[kind, 0], precv_sem.at[kind, slot], me).wait_recv()

    def write(src, kind, b, lanes):
        for a in range(4):
            for j in (0, 1):
                for n in (0, 1):
                    row = n * BINS + kind * 32 + b * 8 + a * 2 + j
                    weights_ref[pl.ds(pl.multiple_of(row * TARGETS, TARGETS), TARGETS), lanes] = src[
                        kind, b * 4 + a, pl.ds((j * 2 + n) * TARGETS, TARGETS), :
                    ]
        for n in (0, 1):
            rows8 = [
                src[kind, b * 4 + a, pl.ds(4 * TARGETS + j * 2 + n, 1), :] for a in range(4) for j in (0, 1)
            ]
            start = pl.multiple_of(n * BINS + kind * 32 + b * 8, 8)
            gains_ref[pl.ds(start, 8), lanes] = jnp.concatenate(rows8, axis=0)

    def to_mate(kind, slot):
        remote(
            pack.at[kind, slot], mate.at[kind, slot], msend_sem.at[kind, slot], mrecv_sem.at[kind, slot], mate_id
        ).start()

    ways = (0, -1, 1, 2)

    def at(kind, i, k):
        a, b = place(kind)
        return step(b, ways[k] * sign) * 4 + step(a, ways[i] * sign)

    for kind in (0, 1):
        a, b = place(kind)
        slot = b * 4 + a
        for zh in range(4):
            pack[kind, slot, pl.ds(zh * TARGETS, TARGETS), :] = share[kind * 4 + zh, 0:TARGETS, :]
            pack[kind, slot, pl.ds(4 * TARGETS + zh, 1), :] = share[kind * 4 + zh, TARGETS : TARGETS + 1, :]
            pack[kind, slot, pl.ds(4 * TARGETS + 4 + zh, 1), :] = share[kind * 4 + zh, TARGETS : TARGETS + 1, :]
        pass_on(kind, slot, device(kind, step(a, sign), b, z), 0)
        pass_on(kind, slot, device(kind, step(a, -sign), b, z), 1)
        pass_on(kind, slot, device(kind, step(a, 2), b, z), 2)

    def across(kind, i):
        a, b = place(kind)
        slot = at(kind, i, 0)
        if i == 3:
            pass_on(kind, slot, device(kind, a, step(b, 2), z), 14)
        pass_on(kind, slot, device(kind, a, step(b, sign), z), 3 + 2 * i)
        pass_on(kind, slot, device(kind, a, step(b, -sign), z), 4 + 2 * i)
        to_mate(kind, slot)

    def onward(i):
        for kind in (0, 1):
            landed(kind, at(kind, i, 1))
            a, b = place(kind)
            pass_on(kind, at(kind, i, 1), device(kind, a, step(b, sign), z), 11 + i)
            to_mate(kind, at(kind, i, 1))

    for kind in (0, 1):
        across(kind, 0)
    for i in (1, 2, 3):
        for kind in (0, 1):
            landed(kind, at(kind, i, 0))
            across(kind, i)
        if i == 2:
            onward(0)
    onward(1)
    onward(2)
    for i, k in ((0, 2), (0, 3), (1, 2), (2, 2), (3, 1), (3, 2), (1, 3), (2, 3), (3, 3)):
        for kind in (0, 1):
            landed(kind, at(kind, i, k))
            to_mate(kind, at(kind, i, k))

    def finish(b, carry):
        for kind in (0, 1):
            write(pack, kind, b, own_lanes)
        return carry

    lax.fori_loop(0, 4, finish, 0)

    def finish_mate(b, carry):
        for kind in (0, 1):
            for a in range(4):
                slot = b * 4 + a
                remote(
                    mate.at[kind, slot], mate.at[kind, slot], msend_sem.at[kind, slot], mrecv_sem.at[kind, slot], me
                ).wait_recv()
            write(mate, kind, b, mate_lanes)
        return carry

    lax.fori_loop(0, 4, finish_mate, 0)

    swap_bins.wait_send()
    swap_vals.wait_send()
    for kind in (0, 1):
        a, b = place(kind)
        for d in (1, 2, 3):
            tl_copy(kind, b, step(b, d)).wait_send()
    for d in range(1, NZ):
        to = (z + d) % NZ
        tz_copy(z, to).wait_send()
        spread_line(z, to, me).wait_send()
        if d % 2 == 0:
            line(to).wait_send()
        else:

            @pl.when(wide(to))
            def _(to=to):
                line(to).wait_send()

    def drain(m, carry):
        for kind in (0, 1):
            one(m, kind, me).wait_send()
            zero(m, kind, me).wait_send()
            remote(pack.at[kind, 0], pack.at[kind, 0], psend_sem.at[kind, m], precv_sem.at[kind, 0], me).wait_send()
        return carry

    lax.fori_loop(0, 15, drain, 0)

    def drain_pairs(m, carry):
        for kind in (0, 1):
            pair(m, kind).wait_send()
            remote(
                pack.at[kind, m], pack.at[kind, m], msend_sem.at[kind, m], mrecv_sem.at[kind, m], me
            ).wait_send()
        return carry

    lax.fori_loop(0, PLANE, drain_pairs, 0)


def on_device(bin_index, node_ids, gradients, hessians):
    rows, features = bin_index.shape
    dma = pltpu.SemaphoreType.DMA
    vmem = pltpu.VMEM
    f32 = jnp.float32
    whole = pl.BlockSpec(memory_space=pltpu.VMEM)
    operands = [bin_index, node_ids.reshape(1, rows), gradients.T, hessians.T]
    weights, gains = pl.pallas_call(
        functools.partial(kernel, rows),
        out_shape=(
            jax.ShapeDtypeStruct((2 * BINS * TARGETS, features), f32),
            jax.ShapeDtypeStruct((2 * BINS, features), f32),
        ),
        in_specs=[pl.BlockSpec(memory_space=pltpu.HBM)] * 4,
        out_specs=(whole, whole),
        scratch_shapes=[
            vmem((1, rows), jnp.int32),
            vmem((TARGETS, rows), jnp.bfloat16),
            vmem((TARGETS, rows), jnp.bfloat16),
            vmem((2 * rows, LANES), jnp.int32),
            vmem((2 * WIDE, 2 * rows), jnp.bfloat16),
            vmem((PIECE, rows), f32),
            vmem((PIECE, rows), f32),
            vmem((EARLY, 2 * WIDE, 4 * LANES), f32),
            vmem((NZ, 8, LANES), f32),
            vmem((2, 4, 8, LANES), f32),
            vmem((4, 2, 2 * WIDE, LANES), f32),
            vmem((16, 2, 2, WIDE, LANES), f32),
            vmem((16, 2, WIDE, LANES), f32),
            vmem((15, 2, 2 * WIDE, LANES), f32),
            vmem((15, 2, 2 * WIDE, LANES), f32),
            vmem((15, 2, WIDE, LANES), f32),
            vmem((15, 2, WIDE, LANES), f32),
            vmem((NZ, WIDE, LANES), f32),
            vmem((NZ, WIDE, LANES), f32),
            vmem((NZ, SHARE, LANES), f32),
            vmem((2, PLANE, PACK, LANES), f32),
            vmem((2, PLANE, PACK, LANES), f32),
            dma((4,)),
            dma((2,)),
            dma((2,)),
            dma((NZ,)),
            dma((NZ,)),
            dma((2, 4)),
            dma((2, 4)),
            dma((16, 2)),
            dma((16, 2)),
            dma((15, 2)),
            dma((15, 2)),
            dma((15, 2)),
            dma((15, 2)),
            dma((NZ,)),
            dma((NZ,)),
            dma((NZ,)),
            dma((NZ,)),
            dma((2, 15)),
            dma((2, PLANE)),
            dma((2, PLANE)),
            dma((2, PLANE)),
        ],
        compiler_params=pltpu.CompilerParams(collective_id=0, has_side_effects=True, vmem_limit_bytes=30 << 20),
        name="level",
    )(*[pltpu.with_memory_space_constraint(v, pltpu.HBM) for v in operands])
    weights = jnp.transpose(weights.reshape(2, BINS, TARGETS, features), (3, 0, 1, 2))
    gains = jnp.transpose(gains.reshape(2, BINS, features), (2, 0, 1))
    return (gains, weights)


def solution(mesh):
    return jax.shard_map(
        on_device,
        mesh=mesh,
        in_specs=(P("dp", None), P("dp"), P("dp", None), P("dp", None)),
        out_specs=(P(), P()),
        check_vma=False,
    )
```

```python
import functools

import jax
import jax.numpy as jnp
from jax import lax
from jax.experimental import pallas as pl
from jax.experimental.pallas import tpu as pltpu
from jax.sharding import PartitionSpec as P

MESH = pl.DeviceIdType.MESH

BINS = 64
TARGETS = 32
WIDE = 2 * TARGETS
LANES = 128
NX, NY, NZ = 4, 4, 8
PLANE = NX * NY
RIDGE = 1.0
DEPTH = 1024
PIECE = WIDE + 8
EARLY = 4
SHARE = TARGETS + 8
PACK = 4 * TARGETS + 8


def offset(u):
    high, low = u // 2, u % 2
    return (2 + low) * (1 - high) + (1 - low) * high


def kernel(
    rows,
    bins_hbm,
    node_hbm,
    grad_hbm,
    hess_hbm,
    weights_ref,
    gains_ref,
    node_ref,
    grad_ref,
    hess_ref,
    bins,
    spread,
    mine,
    theirs,
    early,
    tz,
    tline,
    raw,
    pairs,
    paired,
    sent1,
    got1,
    sent0,
    got0,
    zsent,
    zgot,
    share,
    pack,
    mate,
    own_sem,
    swap_send,
    swap_recv,
    tz_send,
    tz_recv,
    tl_send,
    tl_recv,
    pair_send,
    pair_recv,
    send1,
    recv1,
    send0,
    recv0,
    zsend,
    zrecv,
    ssend_sem,
    srecv_sem,
    psend_sem,
    precv_sem,
    msend_sem,
    mrecv_sem,
):
    me = lax.axis_index("dp")
    core = me % 2
    z = (me // 2) % NZ
    y = (me // (2 * NZ)) % NY
    x = me // (2 * NZ * NY)
    sign = 1 - 2 * core
    other = 1 - core
    mate_id = me + sign
    h = z % 2
    partners = ((z + 1 - 2 * h + NZ) % NZ, (z - 1 + 2 * h + NZ) % NZ)

    def device(kind, a, b, zz):
        xx, yy = (b, a) if kind == 0 else (a, b)
        return ((xx * NY + yy) * NZ + zz) * 2 + core

    def place(kind):
        return (y, x) if kind == 0 else (x, y)

    def step(p, d):
        return (p + d + 8) % 4

    def remote(src, dst, send, recv, target):
        return pltpu.make_async_remote_copy(
            src_ref=src, dst_ref=dst, send_sem=send, recv_sem=recv, device_id=(target,), device_id_type=MESH
        )

    own_lanes = pl.ds(pl.multiple_of(core * LANES, LANES), LANES)
    mate_lanes = pl.ds(pl.multiple_of(other * LANES, LANES), LANES)
    loads = [
        pltpu.make_async_copy(grad_hbm, grad_ref, own_sem.at[0]),
        pltpu.make_async_copy(hess_hbm, hess_ref, own_sem.at[1]),
        pltpu.make_async_copy(node_hbm, node_ref, own_sem.at[2]),
        pltpu.make_async_copy(bins_hbm.at[:, own_lanes], bins.at[pl.ds(0, rows)], own_sem.at[3]),
    ]
    for load in loads:
        load.start()

    barrier = pltpu.get_barrier_semaphore()
    greeted = [mate_id]
    for kind in (0, 1):
        a, b = place(kind)
        greeted += [device(kind, a, step(b, d), z) for d in (1, 2, 3)]
    for d in range(1, NZ):
        greeted.append(device(0, y, x, (z + d) % NZ))
    for peer in greeted:
        pl.semaphore_signal(barrier, inc=1, device_id=(peer,), device_id_type=MESH)

    for load in loads[:3]:
        load.wait()
    mine[0:TARGETS, :] = grad_ref[...].astype(jnp.float32)
    mine[TARGETS:WIDE, :] = hess_ref[...].astype(jnp.float32)
    mine[WIDE:PIECE, :] = jnp.broadcast_to(node_ref[...].astype(jnp.float32), (8, rows))

    pl.semaphore_wait(barrier, len(greeted))

    swap_vals = remote(mine, theirs, swap_send.at[1], swap_recv.at[1], mate_id)
    swap_bins = remote(bins_hbm.at[:, mate_lanes], bins.at[pl.ds(rows, rows)], swap_send.at[0], swap_recv.at[0], mate_id)
    swap_vals.start()
    swap_bins.start()

    def fill(values, start):
        which = values[WIDE : WIDE + 1, :]
        both = values[0:WIDE, :]
        for n in (0, 1):
            part = jnp.where(which == float(n), both, 0.0)
            spread[n * WIDE : (n + 1) * WIDE, start : start + rows] = part.astype(jnp.bfloat16)

    def local(t, u, low, high):
        firsts = []
        for kind in (0, 1):
            a, b = place(kind)
            firsts.append(kind * 32 + step(b, offset(t) * sign) * 8 + step(a, offset(u) * sign) * 2)
        total = None
        for start in range(low, high, DEPTH):
            block = bins[start : start + DEPTH, :]
            hot = [
                jnp.where(block <= first + j, jnp.ones((), jnp.bfloat16), jnp.zeros((), jnp.bfloat16))
                for first in firsts
                for j in (0, 1)
            ]
            term = jnp.dot(
                spread[:, start : start + DEPTH], jnp.concatenate(hot, axis=1), preferred_element_type=jnp.float32
            )
            total = term if total is None else total + term
        return total

    def tz_copy(slot, target):
        return remote(tz.at[slot], tz.at[slot], tz_send.at[target], tz_recv.at[slot], device(0, y, x, target))

    def tl_copy(kind, slot, to):
        a, b = place(kind)
        return remote(
            tline.at[kind, slot], tline.at[kind, slot], tl_send.at[kind, to], tl_recv.at[kind, slot], device(kind, a, to, z)
        )

    def totals_begin():
        ones = jnp.ones((8, 2 * rows), jnp.bfloat16)
        tz[z] = lax.dot_general(ones, spread[...], (((1,), (1,)), ((), ())), preferred_element_type=jnp.float32)
        for d in range(1, NZ):
            tz_copy(z, (z + d) % NZ).start()

    def totals_z():
        value = tz[z]
        for d in range(1, NZ):
            source = (z + d) % NZ
            tz_copy(source, source).wait_recv()
            value = value + tz[source]
        return value

    def totals_line(kind):
        a, b = place(kind)
        value = tline[kind, b]
        for d in (1, 2, 3):
            source = step(b, d)
            tl_copy(kind, source, source).wait_recv()
            value = value + tline[kind, source]
        return value

    def totals_send(kind, value):
        a, b = place(kind)
        tline[kind, b] = value
        for d in (1, 2, 3):
            tl_copy(kind, b, step(b, d)).start()

    def one(m, kind, target):
        return remote(sent1.at[m, kind], got1.at[m, kind], send1.at[m, kind], recv1.at[m, kind], target)

    def zero(m, kind, target):
        return remote(sent0.at[m, kind], got0.at[m, kind], send0.at[m, kind], recv0.at[m, kind], target)

    def pair(i, kind):
        a, b = place(kind)
        return remote(
            pairs.at[i, kind, 1 - h],
            paired.at[i, kind],
            pair_send.at[i, kind],
            pair_recv.at[i, kind],
            device(kind, a, b, partners[kind]),
        )

    toward = (1, -1, 1)

    def extras(t, u):
        if t < 2:
            return []
        if t == 2:
            return [u]
        return [4 + u, 8 + u] + {2: [12], 3: [13, 14]}.get(u, [])

    def target_of(t, u, kind):
        a, b = place(kind)
        if t < 3:
            return device(kind, a, step(b, toward[t] * sign), z)
        return device(kind, step(a, toward[u] * sign), b, z)

    def put1(t, u, kind, value):
        i = t * 4 + u
        last = t == 3 and u == 3
        for e in extras(t, u):
            one(e, kind, me).wait_recv()
            value = value + got1[e, kind]
        if last:
            for n in (0, 1):
                zsent[kind * 4 + 2 + n] = value[n * WIDE : (n + 1) * WIDE, :]
        else:
            sent1[i, kind] = value
            one(i, kind, target_of(t, u, kind)).start()

    def put0(t, u):
        i = t * 4 + u
        last = t == 3 and u == 3
        for kind in (0, 1):
            pair(i, kind).wait_recv()
            value = pairs[i, kind, h] + paired[i, kind]
            for e in extras(t, u):
                zero(e, kind, me).wait_recv()
                value = value + got0[e, kind]
            if last:
                zsent[kind * 4 + h] = value
            else:
                sent0[i, kind] = value
                zero(i, kind, target_of(t, u, kind)).start()

    def late1(u):
        for kind in (0, 1):
            put1(3, u, kind, raw[u, kind])

    def take(t, u, total):
        i = t * 4 + u
        for kind in (0, 1):
            first = total[:, 2 * kind * LANES : (2 * kind + 1) * LANES]
            pairs[i, kind, 0] = first[0:WIDE, :]
            pairs[i, kind, 1] = first[WIDE : 2 * WIDE, :]
            pair(i, kind).start()
            second = total[:, (2 * kind + 1) * LANES : (2 * kind + 2) * LANES]
            if t < 3:
                put1(t, u, kind, second)
            else:
                raw[u, kind] = second

    fill(mine, 0)
    loads[3].wait()
    def begin(u, carry):
        early[u] = local(0, u, 0, rows)
        return carry

    lax.fori_loop(0, EARLY, begin, 0)
    swap_vals.wait_recv()
    fill(theirs, rows)
    swap_bins.wait_recv()

    for t in range(4):

        def stage(u, carry, t=t):
            if t == 0:
                take(0, u, early[u] + local(0, u, rows, 2 * rows))
            else:
                take(t, u, local(t, u, 0, 2 * rows))
                put0(t - 1, u)
            return carry

        lax.fori_loop(0, 2 if t == 3 else 4, stage, 0)
        if t == 0:
            totals_begin()
        if t == 2:
            totals_send(0, totals_z())

    late1(0)
    take(3, 2, local(3, 2, 0, 2 * rows))
    put0(2, 2)
    late1(1)
    take(3, 3, local(3, 3, 0, 2 * rows))
    put0(2, 3)
    put0(3, 0)
    late1(2)
    put0(3, 1)
    totals_send(1, totals_line(0))
    put0(3, 2)
    late1(3)

    def line(to):
        return remote(zsent.at[to], zgot.at[z], zsend.at[to], zrecv.at[z], device(0, y, x, to))

    def wide(zz):
        return (zz // 2) % 2 == 1

    for d in (4, 3, 5, 2, 6, 1, 7):
        to = (z + d) % NZ

        @pl.when(wide(to))
        def _(to=to):
            line(to).start()

    put0(3, 3)
    for d in (4, 2, 6):
        to = (z + d) % NZ

        @pl.when(jnp.logical_not(wide(to)))
        def _(to=to):
            line(to).start()

    everything = totals_line(1)

    def come(d):
        source = (z + d) % NZ
        remote(zsent.at[source], zgot.at[source], zsend.at[source], zrecv.at[source], me).wait_recv()
        return zgot[source]

    @pl.when(wide(z))
    def _():
        value = zsent[z]
        for d in (1, 7, 3, 5):
            value = value + come(d)
        zsent[z] = value

    summed = zsent[z]
    for d in (2, 6, 4):
        summed = summed + come(d)

    row_ids = lax.broadcasted_iota(jnp.int32, (WIDE, LANES), 0)
    lane_ids = lax.broadcasted_iota(jnp.int32, (WIDE, LANES), 1)
    whole = jnp.broadcast_to(everything[0:1, :], (WIDE, LANES))
    column = jnp.sum(jnp.where(row_ids + h * WIDE == lane_ids, whole, 0.0), axis=1, keepdims=True)
    left_g, left_h = summed[0:TARGETS, :], summed[TARGETS:WIDE, :]
    all_g, all_h = column[0:TARGETS, :], column[TARGETS:WIDE, :]
    right_g, right_h = all_g - left_g, all_h - left_h
    score = (
        left_g * left_g / (left_h + RIDGE)
        + right_g * right_g / (right_h + RIDGE)
        - all_g * all_g / (all_h + RIDGE)
    )
    share[z, 0:TARGETS, :] = -left_g / (left_h + RIDGE)
    share[z, TARGETS:SHARE, :] = jnp.broadcast_to(jnp.sum(score, axis=0, keepdims=True) * (1.0 / TARGETS), (8, LANES))

    def spread_line(slot, to, target):
        return remote(share.at[slot], share.at[slot], ssend_sem.at[to], srecv_sem.at[slot], target)

    for d in (4, 3, 5, 2, 6, 1, 7):
        to = (z + d) % NZ
        spread_line(z, to, device(0, y, x, to)).start()
    for d in (1, 7, 2, 6, 3, 5, 4):
        source = (z + d) % NZ
        spread_line(source, source, me).wait_recv()

    def pass_on(kind, slot, target, k):
        remote(
            pack.at[kind, slot], pack.at[kind, slot], psend_sem.at[kind, k], precv_sem.at[kind, slot], target
        ).start()

    def landed(kind, slot):
        remote(pack.at[kind, slot], pack.at[kind, slot], psend_sem.at[kind, 0], precv_sem.at[kind, slot], me).wait_recv()

    def write(src, kind, b, lanes):
        for a in range(4):
            for j in (0, 1):
                for n in (0, 1):
                    row = n * BINS + kind * 32 + b * 8 + a * 2 + j
                    weights_ref[pl.ds(pl.multiple_of(row * TARGETS, TARGETS), TARGETS), lanes] = src[
                        kind, b * 4 + a, pl.ds((j * 2 + n) * TARGETS, TARGETS), :
                    ]
        for n in (0, 1):
            rows8 = [
                src[kind, b * 4 + a, pl.ds(4 * TARGETS + j * 2 + n, 1), :] for a in range(4) for j in (0, 1)
            ]
            start = pl.multiple_of(n * BINS + kind * 32 + b * 8, 8)
            gains_ref[pl.ds(start, 8), lanes] = jnp.concatenate(rows8, axis=0)

    def to_mate(kind, slot):
        remote(
            pack.at[kind, slot], mate.at[kind, slot], msend_sem.at[kind, slot], mrecv_sem.at[kind, slot], mate_id
        ).start()

    ways = (0, -1, 1, 2)

    def at(kind, i, k):
        a, b = place(kind)
        return step(b, ways[k] * sign) * 4 + step(a, ways[i] * sign)

    for kind in (0, 1):
        a, b = place(kind)
        slot = b * 4 + a
        for zh in range(4):
            pack[kind, slot, pl.ds(zh * TARGETS, TARGETS), :] = share[kind * 4 + zh, 0:TARGETS, :]
            pack[kind, slot, pl.ds(4 * TARGETS + zh, 1), :] = share[kind * 4 + zh, TARGETS : TARGETS + 1, :]
            pack[kind, slot, pl.ds(4 * TARGETS + 4 + zh, 1), :] = share[kind * 4 + zh, TARGETS : TARGETS + 1, :]
        pass_on(kind, slot, device(kind, step(a, sign), b, z), 0)
        pass_on(kind, slot, device(kind, step(a, -sign), b, z), 1)
        pass_on(kind, slot, device(kind, step(a, 2), b, z), 2)

    def across(kind, i):
        a, b = place(kind)
        slot = at(kind, i, 0)
        if i == 3:
            pass_on(kind, slot, device(kind, a, step(b, 2), z), 14)
        pass_on(kind, slot, device(kind, a, step(b, sign), z), 3 + 2 * i)
        pass_on(kind, slot, device(kind, a, step(b, -sign), z), 4 + 2 * i)
        to_mate(kind, slot)

    def onward(i):
        for kind in (0, 1):
            landed(kind, at(kind, i, 1))
            a, b = place(kind)
            pass_on(kind, at(kind, i, 1), device(kind, a, step(b, sign), z), 11 + i)
            to_mate(kind, at(kind, i, 1))

    for kind in (0, 1):
        across(kind, 0)
    for i in (1, 2, 3):
        for kind in (0, 1):
            landed(kind, at(kind, i, 0))
            across(kind, i)
        if i == 2:
            onward(0)
    onward(1)
    onward(2)
    for i, k in ((0, 2), (0, 3), (1, 2), (2, 2), (3, 1), (3, 2), (1, 3), (2, 3), (3, 3)):
        for kind in (0, 1):
            landed(kind, at(kind, i, k))
            to_mate(kind, at(kind, i, k))

    def finish(b, carry):
        for kind in (0, 1):
            write(pack, kind, b, own_lanes)
        return carry

    lax.fori_loop(0, 4, finish, 0)

    def finish_mate(b, carry):
        for kind in (0, 1):
            for a in range(4):
                slot = b * 4 + a
                remote(
                    mate.at[kind, slot], mate.at[kind, slot], msend_sem.at[kind, slot], mrecv_sem.at[kind, slot], me
                ).wait_recv()
            write(mate, kind, b, mate_lanes)
        return carry

    lax.fori_loop(0, 4, finish_mate, 0)

    swap_bins.wait_send()
    swap_vals.wait_send()
    for kind in (0, 1):
        a, b = place(kind)
        for d in (1, 2, 3):
            tl_copy(kind, b, step(b, d)).wait_send()
    for d in range(1, NZ):
        to = (z + d) % NZ
        tz_copy(z, to).wait_send()
        spread_line(z, to, me).wait_send()
        if d % 2 == 0:
            line(to).wait_send()
        else:

            @pl.when(wide(to))
            def _(to=to):
                line(to).wait_send()

    def drain(m, carry):
        for kind in (0, 1):
            one(m, kind, me).wait_send()
            zero(m, kind, me).wait_send()
            remote(pack.at[kind, 0], pack.at[kind, 0], psend_sem.at[kind, m], precv_sem.at[kind, 0], me).wait_send()
        return carry

    lax.fori_loop(0, 15, drain, 0)

    def drain_pairs(m, carry):
        for kind in (0, 1):
            pair(m, kind).wait_send()
            remote(
                pack.at[kind, m], pack.at[kind, m], msend_sem.at[kind, m], mrecv_sem.at[kind, m], me
            ).wait_send()
        return carry

    lax.fori_loop(0, PLANE, drain_pairs, 0)


def on_device(bin_index, node_ids, gradients, hessians):
    rows, features = bin_index.shape
    dma = pltpu.SemaphoreType.DMA
    vmem = pltpu.VMEM
    f32 = jnp.float32
    whole = pl.BlockSpec(memory_space=pltpu.VMEM)
    operands = [bin_index, node_ids.reshape(1, rows), gradients.T, hessians.T]
    weights, gains = pl.pallas_call(
        functools.partial(kernel, rows),
        out_shape=(
            jax.ShapeDtypeStruct((2 * BINS * TARGETS, features), f32),
            jax.ShapeDtypeStruct((2 * BINS, features), f32),
        ),
        in_specs=[pl.BlockSpec(memory_space=pltpu.HBM)] * 4,
        out_specs=(whole, whole),
        scratch_shapes=[
            vmem((1, rows), jnp.int32),
            vmem((TARGETS, rows), jnp.bfloat16),
            vmem((TARGETS, rows), jnp.bfloat16),
            vmem((2 * rows, LANES), jnp.int32),
            vmem((2 * WIDE, 2 * rows), jnp.bfloat16),
            vmem((PIECE, rows), f32),
            vmem((PIECE, rows), f32),
            vmem((EARLY, 2 * WIDE, 4 * LANES), f32),
            vmem((NZ, 8, LANES), f32),
            vmem((2, 4, 8, LANES), f32),
            vmem((4, 2, 2 * WIDE, LANES), f32),
            vmem((16, 2, 2, WIDE, LANES), f32),
            vmem((16, 2, WIDE, LANES), f32),
            vmem((15, 2, 2 * WIDE, LANES), f32),
            vmem((15, 2, 2 * WIDE, LANES), f32),
            vmem((15, 2, WIDE, LANES), f32),
            vmem((15, 2, WIDE, LANES), f32),
            vmem((NZ, WIDE, LANES), f32),
            vmem((NZ, WIDE, LANES), f32),
            vmem((NZ, SHARE, LANES), f32),
            vmem((2, PLANE, PACK, LANES), f32),
            vmem((2, PLANE, PACK, LANES), f32),
            dma((4,)),
            dma((2,)),
            dma((2,)),
            dma((NZ,)),
            dma((NZ,)),
            dma((2, 4)),
            dma((2, 4)),
            dma((16, 2)),
            dma((16, 2)),
            dma((15, 2)),
            dma((15, 2)),
            dma((15, 2)),
            dma((15, 2)),
            dma((NZ,)),
            dma((NZ,)),
            dma((NZ,)),
            dma((NZ,)),
            dma((2, 15)),
            dma((2, PLANE)),
            dma((2, PLANE)),
            dma((2, PLANE)),
        ],
        compiler_params=pltpu.CompilerParams(collective_id=0, has_side_effects=True, vmem_limit_bytes=30 << 20),
        name="level",
    )(*[pltpu.with_memory_space_constraint(v, pltpu.HBM) for v in operands])
    weights = jnp.transpose(weights.reshape(2, BINS, TARGETS, features), (3, 0, 1, 2))
    gains = jnp.transpose(gains.reshape(2, BINS, features), (2, 0, 1))
    return (gains, weights)


def solution(mesh):
    return jax.shard_map(
        on_device,
        mesh=mesh,
        in_specs=(P("dp", None), P("dp"), P("dp", None), P("dp", None)),
        out_specs=(P(), P()),
        check_vma=False,
    )
```
